32 devices in a mesh: shards: 4 (over x, core), context: 2 (over y), tensor: 4 (over z).
Axes of the slice: x: 2, y: 2, z: 4, core: 2. Of those that a mesh axis runs over, the one named last changes fastest.
Arguments:
- tokens: bfloat16 [8192, 1280], P(('shards', 'context')), may hold values from -6 to 6
- cotangent: bfloat16 [8192, 1280], P(('shards', 'context')), may hold values from -6 to 6
- segments: int32 [8192], P(('shards', 'context')), may hold values from 0 to 1024, as said below
- positions: int32 [8192], P(('shards', 'context')), may hold values from 0 to 1279, as said below
- w_query: bfloat16 [1280, 1280], P('shards', 'tensor'), may hold values from -0.15625 to 0.15625
- w_key: bfloat16 [1280, 1280], P('shards', 'tensor'), may hold values from -0.15625 to 0.15625
- w_value: bfloat16 [1280, 1280], P('shards', 'tensor'), may hold values from -0.15625 to 0.15625
- w_output: bfloat16 [1280, 1280], P('tensor', 'shards'), may hold values from -0.15625 to 0.15625
- w_up: bfloat16 [1280, 5120], P('shards', 'tensor'), may hold values from -0.15625 to 0.15625
- w_gate: bfloat16 [1280, 5120], P('shards', 'tensor'), may hold values from -0.15625 to 0.15625
- w_down: bfloat16 [5120, 1280], P('tensor', 'shards'), may hold values from -0.078125 to 0.078125
- scale_qk: float32 [1280], P('tensor'), may hold values from 1 to 1.6
- alpha_attn: float32 [1280], replicated, may hold values from 0.15 to 0.6
- alpha_mlp: float32 [1280], replicated, may hold values from 0.15 to 0.6
- scale_up: float32 [5120], P('tensor'), may hold values from 0.25 to 1.75
- scale_gate: float32 [5120], P('tensor'), may hold values from 0.25 to 1.75
Outputs:
- block_out: bfloat16 [8192, 1280], P(('shards', 'context'))
- grad_tokens: bfloat16 [8192, 1280], P(('shards', 'context'))
- grad_query: float32 [1280, 1280], P('shards', 'tensor')
- grad_key: float32 [1280, 1280], P('shards', 'tensor')
- grad_value: float32 [1280, 1280], P('shards', 'tensor')
- grad_output: float32 [1280, 1280], P('tensor', 'shards')
- grad_up: float32 [1280, 5120], P('shards', 'tensor')
- grad_gate: float32 [1280, 5120], P('shards', 'tensor')
- grad_down: float32 [5120, 1280], P('tensor', 'shards')
- grad_scale_qk: float32 [1280], P('tensor')
- grad_alpha_attn: float32 [1280], replicated
- grad_alpha_mlp: float32 [1280], replicated
- grad_scale_up: float32 [5120], P('tensor')
- grad_scale_gate: float32 [5120], P('tensor')
The draws below stay inside these ranges and needn't reach their ends.
Inputs may be any that keep to these rules, and one draw needn't show every extreme that they name: `segments`: each run of 1024 tokens in order (one device of shards and context) holds first 512 prompt tokens (id 0), the prompt's tokens lying in order over the group, then 512 slots filled with whole continuations of 1 to 256 tokens each, one of exactly 256; a continuation's tokens are consecutive and its id is shared by no other continuation of the group. `positions`: A prompt token's position is its index in the group's prompt; a continuation token's is 1024 plus its offset in its continuation.
All inputs are finite; a program needn't handle non-finite values.
Results may differ from the reference program's by a relative error of at most 0.02.
Values may be sent and summed in bfloat16 or wider, within the bound.
No kernel may reach another device: no remote copies, remote signals or barrier semaphores. Data moves between devices by JAX's collectives and lax.ppermute only.
A program may use at most 192 MiB of HBM per device.

```python
import math
import jax
import jax.numpy as jnp
from jax import lax

D = 1280
HEADS = 20
HD = 64
FF = 5120
CONT_DEV = 2
CONT_LEN = 256
PROMPT = 1024
PROMPT_DEV = 512
TOK_DEV = 1024
GROUPS = 4
TOKENS = 8192


def layout(key):
    blocks = TOKENS // TOK_DEV
    per_group = blocks // GROUPS
    slot_count = CONT_DEV * CONT_LEN
    column = jnp.arange(slot_count, dtype=jnp.int32)
    window = column // CONT_LEN
    chosen = jax.random.randint(jax.random.fold_in(key, 23), (blocks, 1), 0, CONT_DEV)
    random_cuts = jax.random.randint(jax.random.fold_in(key, 11), (blocks, slot_count), 0, 48) == 0
    cut_flags = (column % CONT_LEN == 0)[None, :] | random_cuts & (window[None, :] != chosen)
    piece_start = lax.cummax(jnp.where(cut_flags, column[None, :], 0), axis=1)
    following = jnp.concatenate([cut_flags[:, 1:], jnp.ones((blocks, 1), jnp.bool_)], axis=1)
    piece_end = lax.cummin(jnp.where(following, column[None, :], slot_count - 1), axis=1, reverse=True)
    context_index = (jnp.arange(blocks, dtype=jnp.int32) % per_group)[:, None]
    cont_ids = 1 + context_index * slot_count + piece_end
    cont_positions = PROMPT + column[None, :] - piece_start
    prompt_ids = jnp.zeros((blocks, PROMPT_DEV), jnp.int32)
    prompt_positions = context_index * PROMPT_DEV + jnp.arange(PROMPT_DEV, dtype=jnp.int32)[None, :]
    segment_ids = jnp.concatenate([prompt_ids, cont_ids], axis=1).reshape(-1)
    position_ids = jnp.concatenate([prompt_positions, cont_positions], axis=1).reshape(-1)
    return (segment_ids.astype(jnp.int32), position_ids.astype(jnp.int32))


def draw_segments(key, part):
    return layout(jax.random.fold_in(key, 5))[0]


def draw_positions(key, part):
    return layout(jax.random.fold_in(key, 5))[1]


def block_levels(own_key, dims, split, low, high):
    factor_of, own = 1.0, jax.random.fold_in(own_key, 6)
    for position, parts in split:
        steps = jnp.exp(jax.random.uniform(jax.random.fold_in(own, position), (parts,), jnp.float32, low / len(split), high / len(split)))
        factor_of = factor_of * jnp.repeat(steps, dims[position] // parts).reshape([-1 if axis == position else 1 for axis in range(len(dims))])
    return factor_of


def noise(rng, shape, spread, limit, shards=(), kind=jnp.bfloat16):
    drawn = spread * jax.random.normal(rng, shape, jnp.float32)
    if shards:
        drawn = drawn * block_levels(rng, shape, shards, -0.22, 0.18)
    return jnp.clip(drawn, -limit, limit).astype(kind)


def setup_inputs(seed: int = 0) -> dict:
    arg_keys = jax.random.split(jax.random.key(seed), 17)
    tokens = noise(arg_keys[0], (TOKENS, D), 1.0, 6.0, ((0, 8),))
    cotangent = noise(arg_keys[1], (TOKENS, D), 1.0, 6.0, ((0, 8),))
    segments = draw_segments(jax.random.fold_in(arg_keys[16], 71), 0)
    positions = draw_positions(jax.random.fold_in(arg_keys[16], 71), 0)
    w_query = noise(arg_keys[4], (D, D), D ** -0.5, 0.15625, ((0, 4), (1, 4)))
    w_key = noise(arg_keys[5], (D, D), D ** -0.5, 0.15625, ((0, 4), (1, 4)))
    w_value = noise(arg_keys[6], (D, D), D ** -0.5, 0.15625, ((0, 4), (1, 4)))
    w_output = noise(arg_keys[7], (D, D), D ** -0.5, 0.15625, ((0, 4), (1, 4)))
    w_up = noise(arg_keys[8], (D, FF), D ** -0.5, 0.15625, ((0, 4), (1, 4)))
    w_gate = noise(arg_keys[9], (D, FF), D ** -0.5, 0.15625, ((0, 4), (1, 4)))
    w_down = noise(arg_keys[10], (FF, D), FF ** -0.5, 0.078125, ((0, 4), (1, 4)))
    scale_qk = jnp.clip(jnp.exp(math.log(1.6) - 0.47000364 * jax.random.uniform(arg_keys[11], (D,), jnp.float32) ** block_levels(arg_keys[11], (D,), ((0, 4),), -0.2, 0.2)), 1.0, 1.6)
    alpha_attn = jnp.clip(jnp.exp(jax.random.uniform(arg_keys[12], (D,), jnp.float32, math.log(0.15), math.log(0.6))), 0.15, 0.6)
    alpha_mlp = jnp.clip(jnp.exp(jax.random.uniform(arg_keys[13], (D,), jnp.float32, math.log(0.15), math.log(0.6))), 0.15, 0.6)
    scale_up = jnp.clip(1.0 + 0.15 * jax.random.normal(arg_keys[14], (FF,), jnp.float32), 0.25, 1.75)
    scale_gate = jnp.clip(1.0 + 0.15 * jax.random.normal(arg_keys[15], (FF,), jnp.float32), 0.25, 1.75)
    return dict(tokens=tokens, cotangent=cotangent, segments=segments, positions=positions, w_query=w_query, w_key=w_key, w_value=w_value, w_output=w_output, w_up=w_up, w_gate=w_gate, w_down=w_down, scale_qk=scale_qk, alpha_attn=alpha_attn, alpha_mlp=alpha_mlp, scale_up=scale_up, scale_gate=scale_gate)


@jax.custom_vjp
def low(v):
    return lax.optimization_barrier(v.astype(jnp.bfloat16)).astype(jnp.float32)

@jax.custom_vjp
def low_back(v):
    return v

def low_keep(v):
    return (low(v), None)

def low_pass(kept, grad):
    return (grad,)

def back_keep(v):
    return (v, None)

def back_low(kept, grad):
    return (low(grad),)
low.defvjp(low_keep, low_pass)
low_back.defvjp(back_keep, back_low)
EPSILON = 1e-06
MASKED = -1e+30
HIGH = lax.Precision.HIGHEST

def renorm(vector):
    return vector * lax.rsqrt(lax.optimization_barrier(jnp.mean(vector * vector, axis=-1, keepdims=True)) + EPSILON)

def rotate(values, cosine_table, sine_table):
    half_size = values.shape[-1] // 2
    first_half = values[..., :half_size]
    second_half = values[..., half_size:]
    return jnp.concatenate([first_half * cosine_table - second_half * sine_table, second_half * cosine_table + first_half * sine_table], axis=-1)

def head_norm(raw_heads, cosine_table, sine_table, factor):
    turned = rotate(raw_heads, cosine_table[:, None, :], sine_table[:, None, :])
    return factor * turned * lax.rsqrt(lax.optimization_barrier(jnp.sum(turned * turned, axis=-1, keepdims=True)) + EPSILON)

def residual_step(hidden, branch, alpha):
    return renorm(hidden + alpha * (renorm(branch) - hidden))

def swiglu(up_proj, gate_proj, scale_up, scale_gate):
    return scale_up * up_proj * jax.nn.silu(scale_gate * gate_proj)

def phase_tables(positions, head_size):
    half_size = head_size // 2
    frequency = 10000.0 ** (-(jnp.arange(half_size, dtype=jnp.float32) * 2.0 / head_size))
    phases = positions.astype(jnp.float32)[:, None] * frequency[None, :]
    return (jnp.cos(phases), jnp.sin(phases))

def group_attention(operands):
    query_group, key_group, value_group, group_segments, group_positions = operands
    group_size = query_group.shape[0]
    block_count = group_size // TOK_DEV
    multiplier = math.sqrt(HD)

    def query_block(block_operands):
        query_rows, row_segments, row_positions = block_operands
        allowed = (group_positions[None, :] <= row_positions[:, None]) & ((group_segments[None, :] == 0) | (group_segments[None, :] == row_segments[:, None]))
        scores = low_back(multiplier * jnp.einsum('qhd,khd->hqk', query_rows, key_group, precision=HIGH))
        scores = jnp.where(allowed[None], scores, MASKED)
        row_peak = lax.optimization_barrier(jnp.max(scores, axis=-1, keepdims=True))
        weights = jnp.exp(scores - row_peak)
        softmax_weights = weights / lax.optimization_barrier(jnp.sum(weights, axis=-1, keepdims=True))
        return jnp.einsum('hqk,khd->qhd', low(softmax_weights), value_group, precision=HIGH)
    blocks_out = lax.map(jax.checkpoint(query_block), (query_group.reshape(block_count, TOK_DEV, HEADS, HD), group_segments.reshape(block_count, TOK_DEV), group_positions.reshape(block_count, TOK_DEV)))
    return blocks_out.reshape(group_size, HEADS, HD)

def forward(tokens, w_query, w_key, w_value, w_output, w_up, w_gate, w_down, scale_qk, alpha_attn, alpha_mlp, scale_up, scale_gate, segments, positions):
    token_count = tokens.shape[0]
    cosine_table, sine_table = phase_tables(positions, HD)
    factor = scale_qk.reshape(HEADS, HD)
    query_raw = low_back(jnp.dot(tokens, w_query, precision=HIGH)).reshape(token_count, HEADS, HD)
    key_raw = low_back(jnp.dot(tokens, w_key, precision=HIGH)).reshape(token_count, HEADS, HD)
    value_all = low(low_back(jnp.dot(tokens, w_value, precision=HIGH))).reshape(token_count, HEADS, HD)
    query_all = low(head_norm(query_raw, cosine_table, sine_table, factor))
    key_all = low(head_norm(key_raw, cosine_table, sine_table, factor))
    group_shape = (GROUPS, token_count // GROUPS, HEADS, HD)
    mixed = lax.map(group_attention, (query_all.reshape(group_shape), key_all.reshape(group_shape), value_all.reshape(group_shape), segments.reshape(GROUPS, -1), positions.reshape(GROUPS, -1)))
    mixed_low = low(low_back(mixed.reshape(token_count, D)))
    attn_out = low_back(jnp.dot(mixed_low, w_output, precision=HIGH))
    after_attn = residual_step(tokens, attn_out, alpha_attn)
    after_low = low(after_attn)
    up_proj = low_back(jnp.dot(after_low, w_up, precision=HIGH))
    gate_proj = low_back(jnp.dot(after_low, w_gate, precision=HIGH))
    inner_low = low(swiglu(up_proj, gate_proj, scale_up, scale_gate))
    merged = low_back(jnp.dot(inner_low, w_down, precision=HIGH))
    return residual_step(after_attn, merged, alpha_mlp)

def reference(tokens, cotangent, segments, positions, w_query, w_key, w_value, w_output, w_up, w_gate, w_down, scale_qk, alpha_attn, alpha_mlp, scale_up, scale_gate):
    floats = tuple((item.astype(jnp.float32) for item in (tokens, w_query, w_key, w_value, w_output, w_up, w_gate, w_down, scale_qk, alpha_attn, alpha_mlp, scale_up, scale_gate)))

    def wrapped(*inputs):
        return forward(*inputs, segments, positions)
    block_out, pullback = jax.vjp(wrapped, *floats)
    grads = pullback(cotangent.astype(jnp.float32))
    return (block_out.astype(jnp.bfloat16), grads[0].astype(jnp.bfloat16), grads[1], grads[2], grads[3], grads[4], grads[5], grads[6], grads[7], grads[8], grads[9], grads[10], grads[11], grads[12])
```

```python
import functools

import jax
import jax.numpy as jnp
from jax import lax
from jax.experimental import pallas as pl
from jax.experimental.pallas import tpu as pltpu
from jax.sharding import PartitionSpec as P

HD = 64
CONT = 512
BLOCK = 256
EPSILON = 1e-06
BF = jnp.bfloat16
F32 = jnp.float32


def dot(left, right):
    return lax.dot_general(left, right, (((1,), (0,)), ((), ())), preferred_element_type=F32)


def dot_t(left, right):
    return lax.dot_general(left, right, (((1,), (1,)), ((), ())), preferred_element_type=F32)


def outer_sum(left, right):
    return lax.dot_general(left, right, (((0,), (0,)), ((), ())), preferred_element_type=F32)


def renorm(vector):
    return vector * lax.rsqrt(jnp.mean(vector * vector, axis=-1, keepdims=True) + EPSILON)


def residual_step(hidden, branch, alpha):
    return renorm(hidden + alpha * (renorm(branch) - hidden))


def swiglu(up_proj, gate_proj, scale_up, scale_gate):
    return scale_up * up_proj * jax.nn.silu(scale_gate * gate_proj)


def widen(values, lanes):
    pad = lanes - values.shape[1]
    return values if pad == 0 else jnp.concatenate(
        [values, jnp.zeros((values.shape[0], pad), values.dtype)], axis=1
    )


def first_half(shape):
    return lax.broadcasted_iota(jnp.int32, shape, 1) % HD < HD // 2


def swapped(values):
    lanes = values.shape[1]
    after = pltpu.roll(values, lanes - HD // 2, 1)
    before = pltpu.roll(values, HD // 2, 1)
    return jnp.where(first_half(values.shape), -after, before)


def head_sum(values):
    lanes = values.shape[1]
    same = (
        lax.broadcasted_iota(jnp.int32, (lanes, lanes), 0) // HD
        == lax.broadcasted_iota(jnp.int32, (lanes, lanes), 1) // HD
    )
    ones = jnp.where(same, 1.0, 0.0).astype(BF)
    high = values.astype(BF)
    rest = (values - high.astype(F32)).astype(BF)
    return dot(high, ones) + dot(rest, ones)


def table(ref, lanes):
    return jnp.concatenate([ref[...]] * (lanes // 128), axis=1)


def qkv_kernel(tokens, weights, cosine, sine, scale, q_low, k_low, v_low, q_raw, k_raw):
    width = q_low.shape[1]
    lanes = -(-width // 128) * 128
    raw = dot(tokens[...], weights[...])
    cos_full, sin_full = table(cosine, lanes), table(sine, lanes)
    factor = widen(scale[...], lanes)
    for index, (low, kept) in enumerate(((q_low, q_raw), (k_low, k_raw))):
        part = raw[:, index * width : (index + 1) * width]
        kept[...] = part
        wide = widen(part, lanes)
        turned = wide * cos_full + swapped(wide) * sin_full
        normed = factor * turned * lax.rsqrt(head_sum(turned * turned) + EPSILON)
        low[...] = normed[:, :width].astype(BF)
    v_low[...] = raw[:, 2 * width :].astype(BF)


def qkv_call(tokens, weights, cosine, sine, scale):
    rows, model = tokens.shape
    width = weights.shape[1] // 3
    row_spec = lambda n: pl.BlockSpec((BLOCK, n), lambda i: (i, 0))
    whole = lambda shape: pl.BlockSpec(shape, lambda i: (0, 0))
    return pl.pallas_call(
        qkv_kernel,
        grid=(rows // BLOCK,),
        in_specs=[row_spec(model), whole(weights.shape), row_spec(128), row_spec(128), whole((1, width))],
        out_specs=[row_spec(width)] * 5,
        out_shape=[jax.ShapeDtypeStruct((rows, width), BF)] * 3
        + [jax.ShapeDtypeStruct((rows, width), F32)] * 2,
        name="qkv",
    )(tokens, weights, cosine, sine, scale)


def unqkv_kernel(g_q, g_k, g_v, q_raw, k_raw, cosine, sine, scale, g_low, g_scale):
    width = q_raw.shape[1]
    lanes = -(-width // 128) * 128
    cos_full, sin_full = table(cosine, lanes), table(sine, lanes)
    factor = widen(scale[...], lanes)
    parts = []
    total = jnp.zeros((8, lanes), F32)
    for grad_ref, raw_ref in ((g_q, q_raw), (g_k, k_raw)):
        grad, wide = widen(grad_ref[...], lanes), widen(raw_ref[...], lanes)
        turned = wide * cos_full + swapped(wide) * sin_full
        inverse = lax.rsqrt(head_sum(turned * turned) + EPSILON)
        normed = turned * inverse
        total = total + jnp.sum((grad * normed).reshape(-1, 8, lanes), axis=0)
        scaled = grad * factor
        g_turned = inverse * (scaled - normed * head_sum(scaled * normed))
        g_raw = g_turned * cos_full - swapped(g_turned) * sin_full
        parts.append(g_raw[:, :width].astype(BF))
    parts.append(g_v[...].astype(BF))
    g_low[...] = jnp.concatenate(parts, axis=1)
    g_scale[...] = total


def unqkv_call(g_q, g_k, g_v, q_raw, k_raw, cosine, sine, scale):
    rows, width = q_raw.shape
    lanes = -(-width // 128) * 128
    row_spec = lambda n: pl.BlockSpec((BLOCK, n), lambda i: (i, 0))
    return pl.pallas_call(
        unqkv_kernel,
        grid=(rows // BLOCK,),
        in_specs=[row_spec(width)] * 5
        + [row_spec(128), row_spec(128), pl.BlockSpec((1, width), lambda i: (0, 0))],
        out_specs=[row_spec(3 * width), pl.BlockSpec((8, lanes), lambda i: (i, 0))],
        out_shape=[
            jax.ShapeDtypeStruct((rows, 3 * width), BF),
            jax.ShapeDtypeStruct((rows // BLOCK * 8, lanes), F32),
        ],
        name="unqkv",
    )(g_q, g_k, g_v, q_raw, k_raw, cosine, sine, scale)


def take_head(head, heads, pairs, tail=None):
    for index in range(heads):

        @pl.when(head == index)
        def _():
            for source, target in pairs:
                target[:, :HD] = source[:, index * HD : (index + 1) * HD]


def attend_kernel(
    far_open, q, k, v, kf, vf, far_prompt, far_cont, seg_row, seg_col, mixed, total,
    qh, kh, kfh, va, vfa, causal, same,
):
    head = pl.program_id(0)
    heads = q.shape[1] // HD
    prompt = q.shape[0] - CONT

    @pl.when(head == 0)
    def _():
        row = lax.broadcasted_iota(jnp.int32, (prompt, prompt), 0)
        col = lax.broadcasted_iota(jnp.int32, (prompt, prompt), 1)
        causal[...] = jnp.where(row >= col, 1.0, 0.0)
        row = lax.broadcasted_iota(jnp.int32, (CONT, CONT), 0)
        col = lax.broadcasted_iota(jnp.int32, (CONT, CONT), 1)
        same[...] = jnp.where((row >= col) & (seg_col[...] == seg_row[...]), 1.0, 0.0)
        va[...] = jnp.ones(va.shape, BF)
        vfa[...] = jnp.ones(vfa.shape, BF)

    take_head(head, heads, ((q, qh), (k, kh), (v, va), (kf, kfh), (vf, vfa)))
    multiplier = float(HD) ** 0.5
    outs = []
    for start in range(0, prompt + CONT, BLOCK):
        query = qh[start : start + BLOCK, :] * multiplier
        stop = start + BLOCK
        is_prompt = start < prompt
        near = stop if is_prompt else prompt
        weights = jnp.exp(dot_t(query, kh[:near, :]))
        if is_prompt:
            weights = weights * causal[start:stop, :near]
        out = dot(weights.astype(BF), va[:near, :])
        weights = jnp.exp(dot_t(query, kfh[...]))
        if is_prompt:
            weights = weights * far_prompt[...]
        elif not far_open:
            weights = weights * far_cont[...]
        out = out + dot(weights.astype(BF), vfa[...])
        if not is_prompt:
            weights = jnp.exp(dot_t(query, kh[prompt:stop, :]))
            weights = weights * same[start - prompt : stop - prompt, : stop - prompt]
            out = out + dot(weights.astype(BF), va[prompt:stop, :])
        outs.append(out)
    out = jnp.concatenate(outs, axis=0)
    low = (out[:, :HD] / out[:, HD:]).astype(BF)
    sums = out[:, HD:]
    for index in range(heads):

        @pl.when(head == index)
        def _():
            mixed[:, index * HD : (index + 1) * HD] = low
            total[:, index * HD : (index + 1) * HD] = sums


def full_specs(arrays):
    return [pl.BlockSpec(a.shape, lambda h: (0, 0)) for a in arrays]


def attend_call(far_open, q, k, v, kf, vf, far_prompt, far_cont, seg_row, seg_col):
    rows, width = q.shape
    far = kf.shape[0]
    prompt = rows - CONT
    operands = (q, k, v, kf, vf, far_prompt, far_cont, seg_row, seg_col)
    outs = [jax.ShapeDtypeStruct((rows, width), BF), jax.ShapeDtypeStruct((rows, width), F32)]
    return pl.pallas_call(
        functools.partial(attend_kernel, far_open),
        grid=(width // HD,),
        in_specs=full_specs(operands),
        out_specs=full_specs(outs),
        out_shape=outs,
        scratch_shapes=[
            pltpu.VMEM((rows, HD), BF),
            pltpu.VMEM((rows, HD), BF),
            pltpu.VMEM((far, HD), BF),
            pltpu.VMEM((rows, 2 * HD), BF),
            pltpu.VMEM((far, 2 * HD), BF),
            pltpu.VMEM((prompt, prompt), F32),
            pltpu.VMEM((CONT, CONT), F32),
        ],
        name="attend",
    )(*operands)


def unattend_kernel(
    far_open, q, k, v, kf, vf, far_prompt, far_cont, seg_row, seg_col, g_mixed, mixed, total,
    g_q, g_k, g_v, g_kf, g_vf,
    qh, kh, kfh, va, vfa, ga, oh, lh, dq, dk, dv, dkf, dvf, causal, same,
):
    head = pl.program_id(0)
    heads = q.shape[1] // HD
    rows = q.shape[0]
    prompt = rows - CONT
    far = kf.shape[0]

    @pl.when(head == 0)
    def _():
        key = lax.broadcasted_iota(jnp.int32, (BLOCK, BLOCK), 0)
        query = lax.broadcasted_iota(jnp.int32, (BLOCK, BLOCK), 1)
        causal[...] = jnp.where(query >= key, 1.0, 0.0)
        key = lax.broadcasted_iota(jnp.int32, (CONT, CONT), 0)
        query = lax.broadcasted_iota(jnp.int32, (CONT, CONT), 1)
        same[...] = jnp.where((query >= key) & (seg_col[...] == seg_row[...]), 1.0, 0.0)
        va[...] = jnp.ones(va.shape, BF)
        vfa[...] = jnp.ones(vfa.shape, BF)

    take_head(
        head, heads,
        ((q, qh), (k, kh), (v, va), (kf, kfh), (vf, vfa), (g_mixed, ga), (mixed, oh), (total, lh)),
    )
    multiplier = float(HD) ** 0.5
    qh[...] = qh[...] * multiplier
    shared = (ga[:, :HD].astype(F32) / lh[...]).astype(BF)
    drop = -jnp.sum(shared.astype(F32) * oh[...].astype(F32), axis=1, keepdims=True)
    drop_high = drop.astype(BF).astype(F32)
    lane = lax.broadcasted_iota(jnp.int32, (rows, HD), 1)
    tail = jnp.where(lane == 0, drop_high, jnp.where(lane == 1, drop - drop_high, 0.0))
    ga[...] = jnp.concatenate([shared, tail.astype(BF)], axis=1)
    dq[...] = jnp.zeros(dq.shape, F32)

    def tile(keys, values, q0, q1, mask):
        query, grad = qh[q0:q1, :], ga[q0:q1, :]
        weights = jnp.exp(dot_t(keys, query))
        if mask is not None:
            weights = weights * mask
        g_scores = (weights * dot_t(values, grad)).astype(BF)
        dq[q0:q1, :] += outer_sum(g_scores, keys)
        return dot(g_scores, query), dot(weights.astype(BF), grad)[:, :HD]

    def gather(tiles):
        g_key, g_value = tiles[0]
        for more_key, more_value in tiles[1:]:
            g_key, g_value = g_key + more_key, g_value + more_value
        return g_key, g_value

    for start in range(0, rows, BLOCK):
        stop = start + BLOCK
        keys, values = kh[start:stop, :], va[start:stop, :]
        if start < prompt:
            tiles = [tile(keys, values, start, stop, causal[...]), tile(keys, values, stop, rows, None)]
        else:
            mask = same[start - prompt : stop - prompt, start - prompt :]
            tiles = [tile(keys, values, start, rows, mask)]
        dk[start:stop, :], dv[start:stop, :] = gather(tiles)
    for start in range(0, far, CONT):
        stop = min(start + CONT, far)
        keys, values = kfh[start:stop, :], vfa[start:stop, :]
        open_mask = None if far_open else far_cont[start:stop, :]
        tiles = [
            tile(keys, values, 0, prompt, far_prompt[start:stop, :]),
            tile(keys, values, prompt, rows, open_mask),
        ]
        dkf[start:stop, :], dvf[start:stop, :] = gather(tiles)
    for index in range(heads):

        @pl.when(head == index)
        def _():
            lanes = slice(index * HD, (index + 1) * HD)
            g_q[:, lanes] = dq[...] * multiplier
            g_k[:, lanes] = dk[...]
            g_v[:, lanes] = dv[...]
            g_kf[:, lanes] = dkf[...].astype(BF)
            g_vf[:, lanes] = dvf[...].astype(BF)


def unattend_call(far_open, q, k, v, kf, vf, far_prompt, far_cont, seg_row, seg_col, g_mixed, mixed, total):
    rows, width = q.shape
    far = kf.shape[0]
    operands = (q, k, v, kf, vf, far_prompt, far_cont, seg_row, seg_col, g_mixed, mixed, total)
    outs = [jax.ShapeDtypeStruct((rows, width), F32)] * 3 + [jax.ShapeDtypeStruct((far, width), BF)] * 2
    vmem = pltpu.VMEM
    return pl.pallas_call(
        functools.partial(unattend_kernel, far_open),
        grid=(width // HD,),
        in_specs=full_specs(operands),
        out_specs=full_specs(outs),
        out_shape=outs,
        scratch_shapes=[
            vmem((rows, HD), BF),
            vmem((rows, HD), BF),
            vmem((far, HD), BF),
            vmem((rows, 2 * HD), BF),
            vmem((far, 2 * HD), BF),
            vmem((rows, 2 * HD), BF),
            vmem((rows, HD), BF),
            vmem((rows, HD), F32),
            vmem((rows, HD), F32),
            vmem((rows, HD), F32),
            vmem((rows, HD), F32),
            vmem((far, HD), F32),
            vmem((far, HD), F32),
            vmem((BLOCK, BLOCK), F32),
            vmem((CONT, CONT), F32),
        ],
        name="unattend",
    )(*operands)


def after(value, *gates):
    return lax.optimization_barrier((value,) + gates)[0]


def on_device(
    sizes, tokens, cotangent, segments, positions, w_query, w_key, w_value, w_output, w_up, w_gate,
    w_down, scale_qk, alpha_attn, alpha_mlp, scale_up, scale_gate,
):
    n_shards, n_context, n_tensor = sizes
    rows, model = tokens.shape
    prompt = rows - CONT
    chunk = rows // n_tensor
    half = chunk // 2
    width = scale_qk.shape[0]
    shard = lax.axis_index("shards")
    place = lax.axis_index("context")
    lane = lax.axis_index("tensor")

    def flip(value, axis, size, bit):
        return lax.ppermute(value, axis, [(i, i ^ bit) for i in range(size)])

    def total_over(value, axis, size):
        bit = 1
        while bit < size:
            value = value + flip(value, axis, size, bit)
            bit *= 2
        return value

    def shards_gather(own):
        blocks = [(0, own)]
        bit = n_shards // 2
        while bit:
            blocks = blocks + [(k ^ bit, flip(v, "shards", n_shards, bit)) for k, v in blocks]
            bit //= 2
        size = own.shape[0]
        whole = jnp.zeros((n_shards * size, own.shape[1]), own.dtype)
        for k, v in blocks:
            whole = lax.dynamic_update_slice(whole, v, ((shard ^ k) * size, 0))
        return whole

    def shards_sum(whole):
        size = whole.shape[0] // n_shards
        pick = lambda k: lax.dynamic_slice(whole, ((shard ^ k) * size, 0), (size, whole.shape[1]))
        blocks = {k: pick(k) for k in range(n_shards)}
        bit = 1
        while bit < n_shards:
            kept = {}
            for k in blocks:
                if not k & bit:
                    kept[k] = blocks[k] + flip(blocks[k ^ bit].astype(BF), "shards", n_shards, bit).astype(F32)
            blocks = kept
            bit *= 2
        return blocks[0]

    def context_sum(value):
        low = value.astype(BF)
        if n_context == 2:
            return low.astype(F32) + flip(low, "context", n_context, 1).astype(F32)
        part = lax.psum_scatter(low, "context", scatter_dimension=0, tiled=True)
        return lax.all_gather(part, "context", axis=0, tiled=True).astype(F32)

    ring = list(range(0, n_tensor, 2)) + list(range(1, n_tensor, 2))[::-1]
    ring_array = jnp.array(ring, jnp.int32)
    spot = jnp.array([ring.index(i) for i in range(n_tensor)], jnp.int32)[lane]
    forth = [(ring[i], ring[(i + 1) % n_tensor]) for i in range(n_tensor)]
    back = [(b, a) for a, b in forth]
    behind = [ring_array[(spot - j) % n_tensor] * chunk for j in range(n_tensor)]
    ahead = [ring_array[(spot + j) % n_tensor] * chunk + half for j in range(n_tensor)]

    def slot_rows(whole, j):
        cut = lambda start: lax.dynamic_slice(whole, (start, 0), (half, whole.shape[1]))
        return jnp.concatenate([cut(behind[j]), cut(ahead[j])], axis=0)

    def ring_gather(own):
        pairs = [(own[:half], own[half:])]
        for _ in range(n_tensor - 1):
            a, b = pairs[-1]
            pairs.append((lax.ppermute(a, "tensor", forth), lax.ppermute(b, "tensor", back)))
        return pairs

    def ring_sum(slots):
        a, b = slots[1][:half].astype(BF), slots[1][half:].astype(BF)
        for j in list(range(2, n_tensor)) + [0]:
            a = lax.ppermute(a, "tensor", forth).astype(F32) + slots[j][:half]
            b = lax.ppermute(b, "tensor", back).astype(F32) + slots[j][half:]
            if j:
                a, b = a.astype(BF), b.astype(BF)
        return jnp.concatenate([a, b], axis=0)

    def ring_whole(own):
        whole = jnp.zeros((rows, own.shape[1]), own.dtype)
        for j, (a, b) in enumerate(ring_gather(own)):
            whole = lax.dynamic_update_slice(whole, a, (behind[j], 0))
            whole = lax.dynamic_update_slice(whole, b, (ahead[j], 0))
        return whole

    def shift(value, k):
        return lax.ppermute(value, "tensor", [(i, (i + k) % n_tensor) for i in range(n_tensor)])

    weights_qkv = shards_gather(jnp.concatenate([w_query, w_key, w_value], axis=1))
    local_out = jnp.concatenate([w_output] + [shift(w_output, k) for k in range(1, n_tensor)], axis=0)
    frequency = 10000.0 ** (-(jnp.arange(HD // 2, dtype=F32) * 2.0 / HD))
    phases = positions.astype(F32)[:, None] * jnp.tile(frequency, 128 // (HD // 2))[None, :]
    cosine, sine = jnp.cos(phases), jnp.sin(phases)
    scale_row = scale_qk[None, :]
    q_low, k_low, v_low, q_raw, k_raw = qkv_call(tokens, weights_qkv, cosine, sine, scale_row)

    out_local, up_local, gate_local, down_local = lax.optimization_barrier(
        (local_out.T, w_up, w_gate, w_down.T, weights_qkv)
    )[:4]
    out_t = shards_gather(out_local)
    weights_up = shards_gather(up_local)
    weights_gate = shards_gather(gate_local)
    down_t = shards_gather(down_local)

    far_open = n_context == 2
    if far_open:
        k_far = flip(k_low[:prompt], "context", n_context, 1)
        v_far = flip(v_low[:prompt], "context", n_context, 1)
        far_prompt = jnp.full((prompt,), 1.0, F32) * place.astype(F32)
        far_cont = jnp.ones((prompt,), F32)
    else:
        k_far = lax.all_gather(k_low[:prompt], "context", axis=0, tiled=True)
        v_far = lax.all_gather(v_low[:prompt], "context", axis=0, tiled=True)
        owner = jnp.arange(n_context * prompt, dtype=jnp.int32) // prompt
        far_prompt = (owner < place).astype(F32)
        far_cont = (owner != place).astype(F32)
    seg = segments[prompt:]
    mixed, totals = attend_call(
        far_open, q_low, k_low, v_low, k_far, v_far, far_prompt[None, :], far_cont[None, :],
        seg[None, :], seg[:, None],
    )

    def chunk_of(whole, index):
        return lax.dynamic_slice(whole, (index % n_tensor * chunk, 0), (chunk, whole.shape[1]))

    mixed_own = jnp.concatenate(
        [chunk_of(mixed, lane)] + [shift(chunk_of(mixed, lane + k), k) for k in range(1, n_tensor)],
        axis=1,
    )
    attn_out = dot_t(mixed_own, out_t)
    tokens_own = chunk_of(tokens, lane).astype(F32)
    after_attn, attn_back = jax.vjp(residual_step, tokens_own, attn_out, alpha_attn)
    after_pairs = ring_gather(after_attn.astype(BF))
    ups, gates, inners, merged_slots, after_slots = [], [], [], [], []
    for a, b in after_pairs:
        block = jnp.concatenate([a, b], axis=0)
        up, gate = dot(block, weights_up), dot(block, weights_gate)
        inner = swiglu(up, gate, scale_up, scale_gate).astype(BF)
        after_slots.append(block)
        ups.append(up)
        gates.append(gate)
        inners.append(inner)
        merged_slots.append(dot_t(inner, down_t))
    merged = ring_sum(merged_slots)
    block_whole, out_back = jax.vjp(residual_step, after_attn, merged, alpha_mlp)
    block_own = block_whole.astype(BF)
    g_after, g_merged, g_alpha_mlp = out_back(chunk_of(cotangent, lane).astype(F32))
    merged_pairs = ring_gather(g_merged.astype(BF))
    g_merged_slots, g_up_slots, g_gate_slots, g_after_slots = [], [], [], []
    g_scale_up, g_scale_gate = 0.0, 0.0
    for j, (a, b) in enumerate(merged_pairs):
        block = jnp.concatenate([a, b], axis=0)
        _, inner_back = jax.vjp(swiglu, ups[j], gates[j], scale_up, scale_gate)
        g_up, g_gate, more_up, more_gate = inner_back(dot(block, down_t))
        g_up, g_gate = g_up.astype(BF), g_gate.astype(BF)
        g_scale_up, g_scale_gate = g_scale_up + more_up, g_scale_gate + more_gate
        g_merged_slots.append(block)
        g_up_slots.append(g_up)
        g_gate_slots.append(g_gate)
        g_after_slots.append(dot_t(g_up, weights_up) + dot_t(g_gate, weights_gate))
    g_after = g_after + ring_sum(g_after_slots)
    stack = lambda slots: jnp.concatenate(slots, axis=0)
    after_stack = stack(after_slots)
    grad_down_t = shards_sum(outer_sum(stack(g_merged_slots), stack(inners)))
    grad_up = shards_sum(outer_sum(after_stack, stack(g_up_slots)))
    grad_gate = shards_sum(outer_sum(after_stack, stack(g_gate_slots)))

    g_tokens, g_attn, g_alpha_attn = attn_back(g_after)
    g_attn_low = g_attn.astype(BF)
    g_mixed_own = dot(g_attn_low, out_t).astype(BF)
    g_mixed = jnp.zeros((rows, width), BF)
    for k in range(n_tensor):
        part = g_mixed_own[:, k * width : (k + 1) * width]
        part = shift(part, n_tensor - k) if k else part
        g_mixed = lax.dynamic_update_slice(g_mixed, part, ((lane + k) % n_tensor * chunk, 0))
    block_out = ring_whole(after(block_own, g_mixed))
    grad_out_t = shards_sum(outer_sum(g_attn_low, mixed_own)).T
    grad_output = grad_out_t[:width]
    for k in range(1, n_tensor):
        part = grad_out_t[k * width : (k + 1) * width].astype(BF)
        grad_output = grad_output + shift(part, n_tensor - k).astype(F32)

    g_q, g_k, g_v, g_kf, g_vf = unattend_call(
        far_open, q_low, k_low, v_low, k_far, v_far, far_prompt[:, None], far_cont[:, None],
        seg[None, :], seg[:, None], g_mixed, mixed, totals,
    )
    if far_open:
        more_k, more_v = flip(g_kf, "context", n_context, 1), flip(g_vf, "context", n_context, 1)
    else:
        more_k = lax.psum_scatter(g_kf, "context", scatter_dimension=0, tiled=True)
        more_v = lax.psum_scatter(g_vf, "context", scatter_dimension=0, tiled=True)
    g_k = jnp.concatenate([g_k[:prompt] + more_k.astype(F32), g_k[prompt:]], axis=0)
    g_v = jnp.concatenate([g_v[:prompt] + more_v.astype(F32), g_v[prompt:]], axis=0)
    g_qkv, g_scale = unqkv_call(g_q, g_k, g_v, q_raw, k_raw, cosine, sine, scale_row)
    token_slots = [None] * n_tensor
    for j in list(range(1, n_tensor)) + [0]:
        token_slots[j] = dot_t(slot_rows(g_qkv, j), weights_qkv)
    token_sum = ring_sum(token_slots)
    grad_tokens = ring_whole((g_tokens + token_sum).astype(BF))
    grad_qkv = context_sum(shards_sum(outer_sum(tokens, g_qkv)))

    alphas = total_over(jnp.concatenate([g_alpha_attn, g_alpha_mlp]), "tensor", n_tensor)
    small = jnp.concatenate([alphas, g_scale_up, g_scale_gate, jnp.sum(g_scale, axis=0)[:width]])
    small = total_over(total_over(small, "shards", n_shards), "context", n_context)
    hidden = scale_up.shape[0]
    return (
        block_out,
        grad_tokens,
        grad_qkv[:, :width],
        grad_qkv[:, width : 2 * width],
        grad_qkv[:, 2 * width :],
        context_sum(grad_output),
        context_sum(grad_up),
        context_sum(grad_gate),
        context_sum(grad_down_t).T,
        small[2 * model + 2 * hidden :],
        small[:model],
        small[model : 2 * model],
        small[2 * model : 2 * model + hidden],
        small[2 * model + hidden : 2 * model + 2 * hidden],
    )


def solution(mesh):
    sizes = (mesh.shape["shards"], mesh.shape["context"], mesh.shape["tensor"])
    rows = P(("shards", "context"), None)
    row = P(("shards", "context"))
    tall, wide = P("shards", "tensor"), P("tensor", "shards")
    split, copied = P("tensor"), P()
    in_specs = (
        rows, rows, row, row, tall, tall, tall, wide, tall, tall, wide, split, copied, copied, split, split,
    )
    out_specs = (
        rows, rows, tall, tall, tall, wide, tall, tall, wide, split, copied, copied, split, split,
    )
    return jax.shard_map(
        functools.partial(on_device, sizes),
        mesh=mesh,
        in_specs=in_specs,
        out_specs=out_specs,
        check_vma=False,
    )
```
